32 devices in a mesh: row: 8 (over z, x), col: 4 (over y, core).
Axes of the slice: x: 2, y: 2, z: 4, core: 2. Of those that a mesh axis runs over, the one named last changes fastest.
Arguments:
- solution_field: float32 [32, 32768], P(None, ('row', 'col')), may hold values from -6 to 6
- residual: float32 [32, 32768], P(None, ('row', 'col')), may hold values from -420 to 420
- direction: float32 [32, 32768], P(None, ('row', 'col')), may hold values from -420 to 420
- positions: bfloat16 [2, 32768], P(None, ('row', 'col')), may hold values from -6 to 6
- tile_pairs: int32 [2, 49152], P(None, ('row', 'col')), may hold values from 0 to 63, as said below
- pair_count: int32 [32], P(('row', 'col')), may hold values from 0 to 1536, as said below
Outputs:
- solution_next: float32 [32, 32768], P(None, ('row', 'col'))
- residual_next: float32 [32, 32768], P(None, ('row', 'col'))
- direction_next: float32 [32, 32768], P(None, ('row', 'col'))
The draws below stay inside these ranges and needn't reach their ends.
Inputs may be any that keep to these rules, and one draw needn't show every extreme that they name: `tile_pairs`: row 0 holds local row tiles below 32, row 1 local column tiles below 64. The live pairs of one slot block are distinct and strictly upper (I < J); entries in slots that are not live are in range but carry nothing. `pair_count`: some slot block is full in every draw.
All inputs are finite; a program needn't handle non-finite values.
Results may differ from the reference program's by a relative error of at most 0.007.
Values may be sent and summed in bfloat16 or wider, within the bound.
A program may use at most 64 MiB of HBM per device.

```python
import math
import jax
import jax.numpy as jnp
from jax import lax

TILE = 128
PROBES = 32
TILE_DEV = 8
PAIRS_DEV = 1536
NPTS = 32768
N_ROW = 8
N_COL = 4
DEVICES = 32


def pattern_draw(key):
    key_pick = jax.random.fold_in(key, 11)
    key_rank = jax.random.fold_in(key, 12)
    key_full = jax.random.fold_in(key, 13)
    row_span = N_COL * TILE_DEV
    col_span = N_ROW * TILE_DEV
    device = jnp.arange(DEVICES, dtype=jnp.int32)
    row_dev = device // N_COL
    col_dev = device % N_COL
    row_tile = row_dev[:, None] * row_span + jnp.arange(row_span, dtype=jnp.int32)[None, :]
    col_local = jnp.arange(col_span, dtype=jnp.int32)
    col_tile = (col_local[None, :] // TILE_DEV * N_COL + col_dev[:, None]) * TILE_DEV + col_local[None, :] % TILE_DEV
    cell_total = row_span * col_span
    upper_mask = (row_tile[:, :, None] < col_tile[:, None, :]).reshape(DEVICES, cell_total)
    upper_count = jnp.sum(upper_mask.astype(jnp.int32), axis=1)
    levels = jax.random.randint(key_pick, (DEVICES,), 0, 3)
    full_device = jax.random.randint(key_full, (), 0, N_COL)
    levels = jnp.where(device == full_device, 0, levels)
    divisor = jnp.where(levels == 0, 1, jnp.where(levels == 1, 8, 64))
    counts = jnp.minimum(PAIRS_DEV, upper_count // divisor).astype(jnp.int32)
    spread = max(1, 2 ** 30 // cell_total)
    cell_index = jnp.arange(cell_total, dtype=jnp.int32)[None, :]
    scores = jax.random.randint(key_rank, (DEVICES, cell_total), 0, spread) * cell_total + cell_index
    scores = jnp.where(upper_mask, scores, -1 - cell_index)
    ranked, chosen = lax.top_k(scores, PAIRS_DEV)
    pair_table = jnp.stack([chosen // col_span, chosen % col_span]).reshape(2, DEVICES * PAIRS_DEV)
    return (pair_table.astype(jnp.int32), counts)


def draw_tile_pairs(key, part):
    return pattern_draw(key)[0]


def draw_pair_count(key, part):
    return pattern_draw(key)[1]


def probe_draw(key):
    base_part = jnp.clip(jax.random.normal(jax.random.fold_in(key, 21), (PROBES, NPTS), jnp.float32), -5.0, 5.0)
    noise_part = jnp.clip(jax.random.normal(jax.random.fold_in(key, 22), (PROBES, NPTS), jnp.float32), -5.0, 5.0)
    return (base_part, base_part + 0.6 * noise_part)


def draw_residual(key, part):
    return probe_draw(key)[0]


def draw_direction(key, part):
    return probe_draw(key)[1]


def level_of(key, dims, pieces, low, top_value):
    level = 1.0
    for dim, shards_of in pieces:
        steps = jax.random.uniform(jax.random.fold_in(jax.random.fold_in(key, 6), dim), (shards_of,), jnp.float32, low / len(pieces), top_value / len(pieces))
        level = level * jnp.repeat(jnp.exp(steps), dims[dim] // shards_of).reshape((-1,) + (1,) * (len(dims) - 1 - dim))
    return level


def normal_values(key, dims, scale, most, shards=(), kind=jnp.bfloat16):
    level = level_of(key, dims, shards, -0.22, 0.18) if shards else 1.0
    result = jax.random.normal(key, dims, jnp.float32) * scale * level
    return jnp.minimum(jnp.maximum(result, -most), most).astype(kind)


def setup_inputs(seed: int = 0) -> dict:
    key_list = jax.random.split(jax.random.key(seed), 7)
    return {
        "solution_field": normal_values(key_list[0], (PROBES, NPTS), 1.0, 6.0, ((1, 32),), jnp.float32),
        "residual": draw_residual(jax.random.fold_in(key_list[6], 71), 0),
        "direction": draw_direction(jax.random.fold_in(key_list[6], 71), 0),
        "positions": normal_values(key_list[3], (2, NPTS), 1.0, 6.0, ((1, 32),)),
        "tile_pairs": draw_tile_pairs(jax.random.fold_in(key_list[6], 71), 0),
        "pair_count": draw_pair_count(jax.random.fold_in(key_list[6], 71), 0),
    }


AMPLITUDE = 0.025
NUGGET = 2.0
RADIUS = 1.0
HIGHEST = lax.Precision.HIGHEST

def kernel_tile(near_side, far_side):
    differ = near_side[..., :, None] - far_side[..., None, :]
    distance = jnp.sqrt(lax.optimization_barrier(jnp.sum(differ * differ, axis=0))) / RADIUS
    remain = jnp.maximum(1.0 - distance, 0.0)
    return AMPLITUDE * remain ** 4 * (4.0 * distance + 1.0)

def cross_gram_matrix(former, latter):
    return lax.dot_general(former.astype(jnp.float32), latter.astype(jnp.float32), (((1,), (1,)), ((), ())), precision=HIGHEST, preferred_element_type=jnp.float32)

def apply_left(matrix, vectors):
    return jnp.dot(matrix.T, vectors, precision=HIGHEST)

def symmetric_solve(matrix, target):
    balanced = 0.5 * (matrix + matrix.T)
    factor = jnp.linalg.cholesky(balanced)
    middle = lax.linalg.triangular_solve(factor, target, left_side=True, lower=True)
    return lax.linalg.triangular_solve(factor, middle, left_side=True, lower=True, transpose_a=True)

def reference(solution_field, residual, direction, positions, tile_pairs, pair_count):
    tile_count = NPTS // TILE
    dir_half = lax.optimization_barrier(direction.astype(jnp.bfloat16))
    dir_round = dir_half.astype(jnp.float32).reshape(PROBES, tile_count, TILE)
    coords = positions.astype(jnp.float32).reshape(2, tile_count, TILE)
    total = DEVICES * PAIRS_DEV
    entry = jnp.arange(total, dtype=jnp.int32)
    device = entry // PAIRS_DEV
    slot_index = entry % PAIRS_DEV
    row_dev = device // N_COL
    col_dev = device % N_COL
    row_tile = (row_dev * (N_COL * TILE_DEV) + tile_pairs[0]).astype(jnp.int32)
    col_local = tile_pairs[1]
    col_tile = ((col_local // TILE_DEV * N_COL + col_dev) * TILE_DEV + col_local % TILE_DEV).astype(jnp.int32)
    live_mask = slot_index < pair_count[device]
    block_size = math.gcd(total, 256)
    block_count = total // block_size

    def accumulate(running_totals, packed):
        rows_now, cols_now, live_now = packed
        kernel_block = kernel_tile(coords[:, rows_now], coords[:, cols_now])
        kernel_block = jnp.where(live_now[:, None, None], kernel_block, 0.0).astype(jnp.bfloat16)
        kernel_block = lax.optimization_barrier(kernel_block).astype(jnp.float32)
        forward_step = jnp.einsum('bpq,kbq->kbp', kernel_block, dir_round[:, cols_now], precision=HIGHEST)
        backward = jnp.einsum('bpq,kbp->kbq', kernel_block, dir_round[:, rows_now], precision=HIGHEST)
        running_totals = running_totals.at[:, rows_now].add(forward_step)
        running_totals = running_totals.at[:, cols_now].add(backward)
        return (running_totals, None)
    packed = (row_tile.reshape(block_count, block_size), col_tile.reshape(block_count, block_size), live_mask.reshape(block_count, block_size))
    kernel_sum, unused = lax.scan(accumulate, jnp.zeros((PROBES, tile_count, TILE), jnp.float32), packed)
    diagonal = lax.optimization_barrier(kernel_tile(coords, coords).astype(jnp.bfloat16)).astype(jnp.float32)
    kernel_sum = kernel_sum + jnp.einsum('npq,knq->knp', diagonal, dir_round, precision=HIGHEST)
    applied = NUGGET * direction + kernel_sum.reshape(PROBES, NPTS)
    curvature = cross_gram_matrix(direction, applied)
    crossing = cross_gram_matrix(direction, residual)
    norm_old = cross_gram_matrix(residual, residual)
    step_size = symmetric_solve(curvature, crossing)
    solution_next = solution_field + apply_left(step_size, direction)
    residual_next = residual - apply_left(step_size, applied)
    norm_new = cross_gram_matrix(residual_next, residual_next)
    mix_weight = symmetric_solve(norm_old, norm_new)
    direction_next = residual_next + apply_left(mix_weight, direction)
    return (solution_next, residual_next, direction_next)
```

```python
import functools

import jax
import jax.numpy as jnp
from jax import lax
from jax.experimental import pallas as pl
from jax.experimental.pallas import tpu as pltpu
from jax.sharding import PartitionSpec as P

TILE = 128
FEATURES = 16
UNROLL = 4

AMPLITUDE = 0.025
NUGGET = 2.0
RADIUS = 1.0
HIGHEST = lax.Precision.HIGHEST


def cross_gram_matrix(former, latter):
    return lax.dot_general(
        former,
        latter,
        (((1,), (1,)), ((), ())),
        precision=HIGHEST,
        preferred_element_type=jnp.float32,
    )


def apply_left(matrix, vectors):
    return jnp.dot(matrix.T, vectors, precision=HIGHEST)


def symmetric_solve(matrix, target):
    balanced = 0.5 * (matrix + matrix.T)
    factor = jnp.linalg.cholesky(balanced)
    middle = lax.linalg.triangular_solve(factor, target, left_side=True, lower=True)
    return lax.linalg.triangular_solve(factor, middle, left_side=True, lower=True, transpose_a=True)


def split_three(value):
    high = lax.reduce_precision(value, 8, 7)
    rest = value - high
    middle = lax.reduce_precision(rest, 8, 7)
    return high, middle, rest - middle


def features(positions):
    coord = positions.astype(jnp.float32)
    x, y = coord[0], coord[1]
    high, middle, low = split_three(x * x + y * y)
    one = jnp.ones_like(x)
    zero = jnp.zeros_like(x)
    pad = [zero] * (FEATURES - 8)
    near = jnp.stack([x, y, high, middle, low, one, one, one] + pad)
    far = 16.0 * jnp.stack([-2.0 * x, -2.0 * y, one, one, one, high, middle, low] + pad)
    return near.astype(jnp.bfloat16), far.astype(jnp.bfloat16)


def kernel_of(square):
    square = jnp.minimum(jnp.maximum(square, 1e-20), 16.0)
    quad = square * lax.rsqrt(square)
    remain = 4.0 - quad
    remain = remain * remain
    return (remain * remain * (quad + 1.0)).astype(jnp.bfloat16)


def pair_kernel(
    own_tiles, pairs, count, near, far, row_vec, col_vec, row_out, col_out, own_out, row_acc, col_acc
):
    row_acc[...] = jnp.zeros_like(row_acc)
    col_acc[...] = jnp.zeros_like(col_acc)
    scale = AMPLITUDE / 256.0
    live = count[0]

    def products(i, j):
        block = kernel_of(jnp.dot(near[i], far[j], preferred_element_type=jnp.float32))
        forward = lax.dot_general(
            col_vec[j], block, (((1,), (1,)), ((), ())), preferred_element_type=jnp.float32
        )
        backward = jnp.dot(row_vec[i], block, preferred_element_type=jnp.float32)
        return forward, backward

    def several(first, number):
        index = [(pairs[0, first + k], pairs[1, first + k]) for k in range(number)]
        results = [products(i, j) for i, j in index]
        for (i, j), (forward, backward) in zip(index, results):
            row_acc[i] += forward
            col_acc[j] += backward

    whole = live // UNROLL

    @pl.loop(0, whole)
    def _(step):
        several(step * UNROLL, UNROLL)

    @pl.loop(whole * UNROLL, live)
    def _(slot):
        several(slot, 1)

    row_base = lax.axis_index("col") * own_tiles
    col_base = lax.axis_index("row") * own_tiles

    @pl.loop(0, own_tiles)
    def _(t):
        block = kernel_of(
            jnp.dot(near[row_base + t], far[col_base + t], preferred_element_type=jnp.float32)
        )
        own_out[t] = scale * lax.dot_general(
            col_vec[col_base + t],
            block,
            (((1,), (1,)), ((), ())),
            preferred_element_type=jnp.float32,
        )

    row_out[...] = (scale * row_acc[...]).astype(row_out.dtype)
    col_out[...] = (scale * col_acc[...]).astype(col_out.dtype)


def tile_major(array):
    rows, points = array.shape
    return array.reshape(rows, points // TILE, TILE).transpose(1, 0, 2)


def on_device(solution_field, residual, direction, positions, tile_pairs, pair_count):
    probes, own_points = direction.shape
    own_tiles = own_points // TILE
    own_vec = tile_major(direction.astype(jnp.bfloat16))
    near, far = features(positions)
    near = near.reshape(FEATURES, own_tiles, TILE).transpose(1, 2, 0)
    packed = jnp.concatenate([own_vec, tile_major(far)], axis=1)
    col_pack = lax.all_gather(packed, "row", axis=0, tiled=True)
    col_vec, far = col_pack[:, :probes], col_pack[:, probes:]
    row_vec = lax.all_gather(own_vec, "col", axis=0, tiled=True)
    near = lax.all_gather(near, "col", axis=0, tiled=True)
    row_tiles, col_tiles = row_vec.shape[0], col_vec.shape[0]
    vmem = pl.BlockSpec(memory_space=pltpu.VMEM)
    smem = pl.BlockSpec(memory_space=pltpu.SMEM)
    row_part, col_part, own_product = pl.pallas_call(
        functools.partial(pair_kernel, own_tiles),
        out_shape=(
            jax.ShapeDtypeStruct((row_tiles, probes, TILE), jnp.bfloat16),
            jax.ShapeDtypeStruct((col_tiles, probes, TILE), jnp.bfloat16),
            jax.ShapeDtypeStruct((own_tiles, probes, TILE), jnp.float32),
        ),
        in_specs=[smem, smem, vmem, vmem, vmem, vmem],
        out_specs=(vmem, vmem, vmem),
        scratch_shapes=[
            pltpu.VMEM((row_tiles, probes, TILE), jnp.float32),
            pltpu.VMEM((col_tiles, probes, TILE), jnp.float32),
        ],
        name="pairs",
    )(tile_pairs, pair_count, near, far, row_vec, col_vec)
    row_part = lax.psum_scatter(row_part, "col", scatter_dimension=0, tiled=True)
    col_part = lax.psum_scatter(col_part, "row", scatter_dimension=0, tiled=True)
    product = own_product + row_part.astype(jnp.float32) + col_part.astype(jnp.float32)
    applied = NUGGET * direction + product.transpose(1, 0, 2).reshape(probes, own_points)
    curvature, crossing, norm_old, image_resid, square = lax.psum(
        (
            cross_gram_matrix(direction, applied),
            cross_gram_matrix(direction, residual),
            cross_gram_matrix(residual, residual),
            cross_gram_matrix(applied, residual),
            cross_gram_matrix(applied, applied),
        ),
        ("row", "col"),
    )
    step_size = symmetric_solve(curvature, crossing)
    residual_next = residual - apply_left(step_size, applied)
    shifted = jnp.dot(step_size.T, image_resid, precision=HIGHEST)
    quadratic = jnp.dot(
        step_size.T, jnp.dot(square, step_size, precision=HIGHEST), precision=HIGHEST
    )
    norm_new = norm_old - shifted - shifted.T + quadratic
    solution_next = solution_field + apply_left(step_size, direction)
    mix_weight = symmetric_solve(norm_old, norm_new)
    direction_next = residual_next + apply_left(mix_weight, direction)
    return (solution_next, residual_next, direction_next)


def solution(mesh):
    whole = P(None, ("row", "col"))
    return jax.shard_map(
        on_device,
        mesh=mesh,
        in_specs=(whole, whole, whole, whole, whole, P(("row", "col"))),
        out_specs=(whole, whole, whole),
        check_vma=False,
    )
```

```python
import jax
import jax.numpy as jnp
from jax import lax
from jax.experimental import pallas as pl
from jax.experimental.pallas import tpu as pltpu
from jax.sharding import PartitionSpec as P

TILE = 128
FEATURES = 16
UNROLL = 2
BLOCK = 2 * TILE

AMPLITUDE = 0.025
NUGGET = 2.0
RADIUS = 1.0
HIGHEST = lax.Precision.HIGHEST


def cross_gram_matrix(former, latter):
    return lax.dot_general(
        former,
        latter,
        (((1,), (1,)), ((), ())),
        precision=HIGHEST,
        preferred_element_type=jnp.float32,
    )


def apply_left(matrix, vectors):
    return jnp.dot(matrix.T, vectors, precision=HIGHEST)


def symmetric_solve(matrix, target):
    balanced = 0.5 * (matrix + matrix.T)
    factor = jnp.linalg.cholesky(balanced)
    middle = lax.linalg.triangular_solve(factor, target, left_side=True, lower=True)
    return lax.linalg.triangular_solve(factor, middle, left_side=True, lower=True, transpose_a=True)


def split_three(value):
    high = lax.reduce_precision(value, 8, 7)
    rest = value - high
    middle = lax.reduce_precision(rest, 8, 7)
    return high, middle, rest - middle


def features(positions):
    coord = positions.astype(jnp.float32)
    x, y = coord[0], coord[1]
    high, middle, low = split_three(x * x + y * y)
    one = jnp.ones_like(x)
    zero = jnp.zeros_like(x)
    pad = [zero] * (FEATURES - 8)
    near = jnp.stack([x, y, high, middle, low, one, one, one] + pad)
    far = 16.0 * jnp.stack([-2.0 * x, -2.0 * y, one, one, one, high, middle, low] + pad)
    return near.astype(jnp.bfloat16), far.astype(jnp.bfloat16)


def kernel_of(square, floor):
    square = jnp.minimum(jnp.maximum(square, floor), 16.0)
    quad = square * lax.rsqrt(square)
    remain = 4.0 - quad
    remain = remain * remain
    return (remain * remain * (quad + 1.0)).astype(jnp.bfloat16)


def block_of(near, far, floors):
    square = jnp.dot(near, far, preferred_element_type=jnp.float32)
    rows = []
    for a in range(2):
        part = square[a * TILE : (a + 1) * TILE]
        row = [kernel_of(part[:, b * TILE : (b + 1) * TILE], floors[a][b]) for b in range(2)]
        rows.append(jnp.concatenate(row, axis=1))
    return jnp.concatenate(rows, axis=0)


def times_transposed(vectors, block):
    return lax.dot_general(
        vectors, block, (((1,), (1,)), ((), ())), preferred_element_type=jnp.float32
    )


def pair_kernel(
    pairs, count, near, far, row_vec, col_vec, row_out, col_out, own_out, col_acc, floor
):
    row_blocks, col_blocks = near.shape[0], far.shape[0]
    own_blocks = own_out.shape[0]
    stride = 2 * col_blocks
    scale = AMPLITUDE / 256.0
    live = count[0]
    col_acc[...] = jnp.zeros_like(col_acc)

    @pl.loop(0, 2 * row_blocks * stride // 16)
    def _(step):
        for k in range(16):
            floor[step * 16 + k] = 16.0

    def mark(slot):
        floor[pairs[0, slot] * stride + pairs[1, slot]] = 1e-20

    whole = live // 8

    @pl.loop(0, whole)
    def _(step):
        for k in range(8):
            mark(step * 8 + k)

    @pl.loop(whole * 8, live)
    def _(slot):
        mark(slot)

    def products(i, j):
        base = 2 * i * stride + 2 * j
        floors = [[floor[base + a * stride + b] for b in range(2)] for a in range(2)]
        block = block_of(near[i], far[j], floors)
        forward = times_transposed(col_vec[j], block)
        backward = jnp.dot(row_vec[i], block, preferred_element_type=jnp.float32)
        return forward, backward

    @pl.loop(0, row_blocks)
    def _(i):
        def several(step, total):
            results = [products(i, step * UNROLL + k) for k in range(UNROLL)]
            for k, (forward, backward) in enumerate(results):
                total = total + forward
                col_acc[step * UNROLL + k] += backward
            return total

        start = jnp.zeros(row_vec.shape[1:], jnp.float32)
        total = lax.fori_loop(0, col_blocks // UNROLL, several, start)
        row_out[i] = (scale * total).astype(row_out.dtype)

    row_base = lax.axis_index("col") * own_blocks
    col_base = lax.axis_index("row") * own_blocks

    @pl.loop(0, own_blocks)
    def _(t):
        block = block_of(near[row_base + t], far[col_base + t], [[1e-20, 16.0], [16.0, 1e-20]])
        own_out[t] = scale * times_transposed(col_vec[col_base + t], block)

    col_out[...] = (scale * col_acc[...]).astype(col_out.dtype)


def block_major(array):
    rows, points = array.shape
    return array.reshape(rows, points // BLOCK, BLOCK).transpose(1, 0, 2)


def on_device(solution_field, residual, direction, positions, tile_pairs, pair_count):
    probes, own_points = direction.shape
    own_blocks = own_points // BLOCK
    own_vec = block_major(direction.astype(jnp.bfloat16))
    near, far = features(positions)
    near = near.reshape(FEATURES, own_blocks, BLOCK).transpose(1, 2, 0)
    packed = jnp.concatenate([own_vec, block_major(far)], axis=1)
    col_pack = lax.all_gather(packed, "row", axis=0, tiled=True)
    col_vec, far = col_pack[:, :probes], col_pack[:, probes:]
    row_vec = lax.all_gather(own_vec, "col", axis=0, tiled=True)
    near = lax.all_gather(near, "col", axis=0, tiled=True)
    row_blocks, col_blocks = row_vec.shape[0], col_vec.shape[0]
    vmem = pl.BlockSpec(memory_space=pltpu.VMEM)
    smem = pl.BlockSpec(memory_space=pltpu.SMEM)
    row_part, col_part, own_product = pl.pallas_call(
        pair_kernel,
        out_shape=(
            jax.ShapeDtypeStruct((row_blocks, probes, BLOCK), jnp.bfloat16),
            jax.ShapeDtypeStruct((col_blocks, probes, BLOCK), jnp.bfloat16),
            jax.ShapeDtypeStruct((own_blocks, probes, BLOCK), jnp.float32),
        ),
        in_specs=[smem, smem, vmem, vmem, vmem, vmem],
        out_specs=(vmem, vmem, vmem),
        scratch_shapes=[
            pltpu.VMEM((col_blocks, probes, BLOCK), jnp.float32),
            pltpu.SMEM((4 * row_blocks * col_blocks,), jnp.float32),
        ],
        name="pairs",
    )(tile_pairs, pair_count, near, far, row_vec, col_vec)
    row_part = lax.psum_scatter(row_part, "col", scatter_dimension=0, tiled=True)
    col_part = lax.psum_scatter(col_part, "row", scatter_dimension=0, tiled=True)
    product = own_product + row_part.astype(jnp.float32) + col_part.astype(jnp.float32)
    applied = NUGGET * direction + product.transpose(1, 0, 2).reshape(probes, own_points)
    curvature, crossing, norm_old, image_resid, square = lax.psum(
        (
            cross_gram_matrix(direction, applied),
            cross_gram_matrix(direction, residual),
            cross_gram_matrix(residual, residual),
            cross_gram_matrix(applied, residual),
            cross_gram_matrix(applied, applied),
        ),
        ("row", "col"),
    )
    step_size = symmetric_solve(curvature, crossing)
    residual_next = residual - apply_left(step_size, applied)
    shifted = jnp.dot(step_size.T, image_resid, precision=HIGHEST)
    quadratic = jnp.dot(
        step_size.T, jnp.dot(square, step_size, precision=HIGHEST), precision=HIGHEST
    )
    norm_new = norm_old - shifted - shifted.T + quadratic
    solution_next = solution_field + apply_left(step_size, direction)
    mix_weight = symmetric_solve(norm_old, norm_new)
    direction_next = residual_next + apply_left(mix_weight, direction)
    return (solution_next, residual_next, direction_next)


def solution(mesh):
    whole = P(None, ("row", "col"))
    return jax.shard_map(
        on_device,
        mesh=mesh,
        in_specs=(whole, whole, whole, whole, whole, P(("row", "col"))),
        out_specs=(whole, whole, whole),
        check_vma=False,
    )
```

```python
import functools

import jax
import jax.numpy as jnp
from jax import lax
from jax.experimental import pallas as pl
from jax.experimental.pallas import tpu as pltpu
from jax.sharding import PartitionSpec as P

TILE = 128
FEATURES = 16
UNROLL = 2
BLOCK = 2 * TILE

AMPLITUDE = 0.025
NUGGET = 2.0
RADIUS = 1.0
HIGHEST = lax.Precision.HIGHEST


def cross_gram_matrix(former, latter):
    return lax.dot_general(
        former,
        latter,
        (((1,), (1,)), ((), ())),
        precision=HIGHEST,
        preferred_element_type=jnp.float32,
    )


def apply_left(matrix, vectors):
    return jnp.dot(matrix.T, vectors, precision=HIGHEST)


def symmetric_solve(matrix, target):
    balanced = 0.5 * (matrix + matrix.T)
    factor = jnp.linalg.cholesky(balanced)
    middle = lax.linalg.triangular_solve(factor, target, left_side=True, lower=True)
    return lax.linalg.triangular_solve(factor, middle, left_side=True, lower=True, transpose_a=True)


def split_three(value):
    high = lax.reduce_precision(value, 8, 7)
    rest = value - high
    middle = lax.reduce_precision(rest, 8, 7)
    return high, middle, rest - middle


def features(positions):
    coord = positions.astype(jnp.float32)
    x, y = coord[0], coord[1]
    high, middle, low = split_three(x * x + y * y)
    one = jnp.ones_like(x)
    zero = jnp.zeros_like(x)
    pad = [zero] * (FEATURES - 8)
    near = jnp.stack([x, y, high, middle, low, one, one, one] + pad)
    far = 16.0 * jnp.stack([-2.0 * x, -2.0 * y, one, one, one, high, middle, low] + pad)
    return near.astype(jnp.bfloat16), far.astype(jnp.bfloat16)


def kernel_of(square, floor):
    square = jnp.minimum(jnp.maximum(square, floor), 16.0)
    quad = square * lax.rsqrt(square)
    remain = 4.0 - quad
    remain = remain * remain
    return (remain * remain * (quad + 1.0)).astype(jnp.bfloat16)


def block_of(near, far, floors):
    square = jnp.dot(near, far, preferred_element_type=jnp.float32)
    rows = []
    for a in range(2):
        part = square[a * TILE : (a + 1) * TILE]
        row = [kernel_of(part[:, b * TILE : (b + 1) * TILE], floors[a][b]) for b in range(2)]
        rows.append(jnp.concatenate(row, axis=1))
    return jnp.concatenate(rows, axis=0)


def times_transposed(vectors, block):
    return lax.dot_general(
        vectors, block, (((1,), (1,)), ((), ())), preferred_element_type=jnp.float32
    )


def pair_kernel(
    pairs, count, near, far, row_vec, col_vec, row_out, col_out, own_out, col_acc, floor
):
    row_blocks, col_blocks = near.shape[0], far.shape[0]
    own_blocks = own_out.shape[0]
    stride = 2 * col_blocks
    scale = AMPLITUDE / 256.0
    live = count[0]
    col_acc[...] = jnp.zeros_like(col_acc)

    @pl.loop(0, 2 * row_blocks * stride // 16)
    def _(step):
        for k in range(16):
            floor[step * 16 + k] = 16.0

    def mark(slot):
        floor[pairs[0, slot] * stride + pairs[1, slot]] = 1e-20

    whole = live // 8

    @pl.loop(0, whole)
    def _(step):
        for k in range(8):
            mark(step * 8 + k)

    @pl.loop(whole * 8, live)
    def _(slot):
        mark(slot)

    def products(i, j):
        base = 2 * i * stride + 2 * j
        floors = [[floor[base + a * stride + b] for b in range(2)] for a in range(2)]
        block = block_of(near[i], far[j], floors)
        forward = times_transposed(col_vec[j], block)
        backward = jnp.dot(row_vec[i], block, preferred_element_type=jnp.float32)
        return forward, backward

    @pl.loop(0, row_blocks)
    def _(i):
        def several(step, total):
            results = [products(i, step * UNROLL + k) for k in range(UNROLL)]
            for k, (forward, backward) in enumerate(results):
                total = total + forward
                col_acc[step * UNROLL + k] += backward
            return total

        start = jnp.zeros(row_vec.shape[1:], jnp.float32)
        total = lax.fori_loop(0, col_blocks // UNROLL, several, start)
        row_out[i] = (scale * total).astype(row_out.dtype)

    row_base = lax.axis_index("col") * own_blocks
    col_base = lax.axis_index("row") * own_blocks

    @pl.loop(0, own_blocks)
    def _(t):
        block = block_of(near[row_base + t], far[col_base + t], [[1e-20, 16.0], [16.0, 1e-20]])
        own_out[t] = scale * times_transposed(col_vec[col_base + t], block)

    col_out[...] = (scale * col_acc[...]).astype(col_out.dtype)


MESH = pl.DeviceIdType.MESH


def greet(sizes):
    barrier = pltpu.get_barrier_semaphore()
    for axis, size in sizes:
        me = lax.axis_index(axis)
        for k in range(1, size):
            peer = lax.rem(me + k, size)
            pl.semaphore_signal(barrier, inc=1, device_id={axis: peer}, device_id_type=MESH)
    pl.semaphore_wait(barrier, sum(size - 1 for _, size in sizes))


class Exchange:
    def __init__(self, axis, size, source, landing, send_sem, recv_sem):
        self.axis, self.size, self.source, self.landing = axis, size, source, landing
        self.send_sem, self.recv_sem = send_sem, recv_sem
        self.me = lax.axis_index(axis)

    def copy(self, k, source, slot, peer):
        return pltpu.make_async_remote_copy(
            src_ref=source,
            dst_ref=self.landing.at[slot],
            send_sem=self.send_sem.at[k],
            recv_sem=self.recv_sem.at[k],
            device_id={self.axis: peer},
            device_id_type=MESH,
        )

    def outgoing(self, k):
        peer = lax.rem(self.me + k, self.size)
        return self.copy(k, self.source(peer), self.me, peer)

    def start(self):
        for k in range(1, self.size):
            self.outgoing(k).start()

    def wait_recv(self):
        for k in range(1, self.size):
            origin = lax.rem(self.me + self.size - k, self.size)
            self.copy(k, self.landing.at[origin], origin, origin).wait_recv()

    def wait_send(self):
        for k in range(1, self.size):
            self.outgoing(k).wait_send()


def gather_kernel(
    n_row, n_col, row_in, col_in, row_out, col_out, own_sem, row_send, row_recv, col_send, col_recv
):
    row_me, col_me = lax.axis_index("col"), lax.axis_index("row")
    own = [
        pltpu.make_async_copy(row_in, row_out.at[row_me], own_sem.at[0]),
        pltpu.make_async_copy(col_in, col_out.at[col_me], own_sem.at[1]),
    ]
    for copy in own:
        copy.start()
    greet((("row", n_row), ("col", n_col)))
    over_row = Exchange("row", n_row, lambda peer: col_in, col_out, col_send, col_recv)
    over_col = Exchange("col", n_col, lambda peer: row_in, row_out, row_send, row_recv)
    over_row.start()
    over_col.start()
    for copy in own:
        copy.wait()
    for exchange in (over_col, over_row):
        exchange.wait_recv()
        exchange.wait_send()


def image_kernel(
    n_row,
    n_col,
    row_part,
    col_part,
    own_product,
    direction,
    residual,
    applied,
    gram,
    row_land,
    col_land,
    gram_own,
    gram_half,
    gram_col,
    gram_row,
    *sems,
):
    blocks = own_product.shape[0]
    row_me, col_me = lax.axis_index("col"), lax.axis_index("row")
    greet((("row", n_row), ("col", n_col)))

    def part_of(parts):
        return lambda peer: parts.at[pl.ds(peer * blocks, blocks)]

    over_row = Exchange("row", n_row, part_of(col_part), col_land, sems[0], sems[1])
    over_col = Exchange("col", n_col, part_of(row_part), row_land, sems[2], sems[3])
    over_row.start()
    over_col.start()
    total = own_product[...]
    total += row_part[pl.ds(row_me * blocks, blocks)].astype(jnp.float32)
    total += col_part[pl.ds(col_me * blocks, blocks)].astype(jnp.float32)
    over_col.wait_recv()
    for k in range(1, n_col):
        total += row_land[lax.rem(row_me + k, n_col)].astype(jnp.float32)
    over_row.wait_recv()
    for k in range(1, n_row):
        total += col_land[lax.rem(col_me + k, n_row)].astype(jnp.float32)
    flat = jnp.concatenate([total[b] for b in range(blocks)], axis=1)
    image = NUGGET * direction[...] + flat
    applied[...] = image
    left = jnp.concatenate([image, residual[...]], axis=0)
    right = jnp.concatenate([left, direction[...]], axis=0)
    product = cross_gram_matrix(left, right)
    lanes = gram_own.shape[1] - product.shape[1]
    gram_own[...] = jnp.concatenate(
        [product, jnp.zeros((product.shape[0], lanes), jnp.float32)], axis=1
    )
    gram_over_col = Exchange("col", n_col, lambda peer: gram_own, gram_col, sems[4], sems[5])
    gram_over_col.start()
    gram_over_col.wait_recv()
    half = gram_own[...]
    for k in range(1, n_col):
        half += gram_col[lax.rem(row_me + k, n_col)]
    gram_half[...] = half
    gram_over_row = Exchange("row", n_row, lambda peer: gram_half, gram_row, sems[6], sems[7])
    gram_over_row.start()
    gram_over_row.wait_recv()
    whole = gram_half[...]
    for k in range(1, n_row):
        whole += gram_row[lax.rem(col_me + k, n_row)]
    gram[...] = whole
    for exchange in (over_row, over_col, gram_over_col, gram_over_row):
        exchange.wait_send()


def block_major(array):
    rows, points = array.shape
    return array.reshape(rows, points // BLOCK, BLOCK).transpose(1, 0, 2)


def on_device(solution_field, residual, direction, positions, tile_pairs, pair_count):
    probes, own_points = direction.shape
    own_blocks = own_points // BLOCK
    own_vec = block_major(direction.astype(jnp.bfloat16))
    near, far = features(positions)
    n_row, n_col = lax.axis_size("row"), lax.axis_size("col")
    vmem = pl.BlockSpec(memory_space=pltpu.VMEM)
    smem = pl.BlockSpec(memory_space=pltpu.SMEM)
    hbm = pl.BlockSpec(memory_space=pl.ANY)
    row_sem, col_sem = pltpu.SemaphoreType.DMA((n_col,)), pltpu.SemaphoreType.DMA((n_row,))
    row_in = jnp.concatenate([own_vec, block_major(near)], axis=1)
    col_in = jnp.concatenate([own_vec, block_major(far)], axis=1)
    row_pack, col_pack = pl.pallas_call(
        functools.partial(gather_kernel, n_row, n_col),
        out_shape=(
            jax.ShapeDtypeStruct((n_col, *row_in.shape), jnp.bfloat16),
            jax.ShapeDtypeStruct((n_row, *col_in.shape), jnp.bfloat16),
        ),
        in_specs=[vmem, vmem],
        out_specs=(hbm, hbm),
        scratch_shapes=[pltpu.SemaphoreType.DMA((2,)), row_sem, row_sem, col_sem, col_sem],
        compiler_params=pltpu.CompilerParams(collective_id=0, has_side_effects=True),
        name="gather",
    )(row_in, col_in)
    row_pack = row_pack.reshape(-1, *row_in.shape[1:])
    col_pack = col_pack.reshape(-1, *col_in.shape[1:])
    row_vec, near = row_pack[:, :probes], row_pack[:, probes:].transpose(0, 2, 1)
    col_vec, far = col_pack[:, :probes], col_pack[:, probes:]
    row_blocks, col_blocks = row_vec.shape[0], col_vec.shape[0]
    row_part, col_part, own_product = pl.pallas_call(
        pair_kernel,
        out_shape=(
            jax.ShapeDtypeStruct((row_blocks, probes, BLOCK), jnp.bfloat16),
            jax.ShapeDtypeStruct((col_blocks, probes, BLOCK), jnp.bfloat16),
            jax.ShapeDtypeStruct((own_blocks, probes, BLOCK), jnp.float32),
        ),
        in_specs=[smem, smem, vmem, vmem, vmem, vmem],
        out_specs=(vmem, vmem, vmem),
        scratch_shapes=[
            pltpu.VMEM((col_blocks, probes, BLOCK), jnp.float32),
            pltpu.SMEM((4 * row_blocks * col_blocks,), jnp.float32),
        ],
        name="pairs",
    )(tile_pairs, pair_count, near, far, row_vec, col_vec)
    applied, gram = pl.pallas_call(
        functools.partial(image_kernel, n_row, n_col),
        out_shape=(
            jax.ShapeDtypeStruct((probes, own_points), jnp.float32),
            jax.ShapeDtypeStruct((2 * probes, TILE), jnp.float32),
        ),
        in_specs=[vmem] * 5,
        out_specs=(vmem, vmem),
        scratch_shapes=[
            pltpu.VMEM((n_col, *own_product.shape), jnp.bfloat16),
            pltpu.VMEM((n_row, *own_product.shape), jnp.bfloat16),
            pltpu.VMEM((2 * probes, TILE), jnp.float32),
            pltpu.VMEM((2 * probes, TILE), jnp.float32),
            pltpu.VMEM((n_col, 2 * probes, TILE), jnp.float32),
            pltpu.VMEM((n_row, 2 * probes, TILE), jnp.float32),
            col_sem,
            col_sem,
            row_sem,
            row_sem,
            row_sem,
            row_sem,
            col_sem,
            col_sem,
        ],
        compiler_params=pltpu.CompilerParams(collective_id=1, has_side_effects=True),
        name="image",
    )(row_part, col_part, own_product, direction, residual)
    square, image_resid = gram[:probes, :probes], gram[:probes, probes : 2 * probes]
    norm_old = gram[probes:, probes : 2 * probes]
    curvature = gram[:probes, 2 * probes : 3 * probes].T
    crossing = gram[probes:, 2 * probes : 3 * probes].T
    step_size = symmetric_solve(curvature, crossing)
    residual_next = residual - apply_left(step_size, applied)
    shifted = jnp.dot(step_size.T, image_resid, precision=HIGHEST)
    quadratic = jnp.dot(
        step_size.T, jnp.dot(square, step_size, precision=HIGHEST), precision=HIGHEST
    )
    norm_new = norm_old - shifted - shifted.T + quadratic
    solution_next = solution_field + apply_left(step_size, direction)
    mix_weight = symmetric_solve(norm_old, norm_new)
    direction_next = residual_next + apply_left(mix_weight, direction)
    return (solution_next, residual_next, direction_next)


def solution(mesh):
    whole = P(None, ("row", "col"))
    return jax.shard_map(
        on_device,
        mesh=mesh,
        in_specs=(whole, whole, whole, whole, whole, P(("row", "col"))),
        out_specs=(whole, whole, whole),
        check_vma=False,
    )
```

```python
import functools
import math

import jax
import jax.numpy as jnp
from jax import lax
from jax.experimental import pallas as pl
from jax.experimental.pallas import tpu as pltpu
from jax.sharding import PartitionSpec as P

TILE = 128
FEATURES = 16
UNROLL = 8
BLOCK = 2 * TILE

AMPLITUDE = 0.025
NUGGET = 2.0
RADIUS = 1.0
HIGHEST = lax.Precision.HIGHEST


def cross_gram_matrix(former, latter):
    return lax.dot_general(
        former,
        latter,
        (((1,), (1,)), ((), ())),
        precision=HIGHEST,
        preferred_element_type=jnp.float32,
    )


def apply_left(matrix, vectors):
    return jnp.dot(matrix.T, vectors, precision=HIGHEST)


def symmetric_solve(matrix, target):
    balanced = 0.5 * (matrix + matrix.T)
    factor = jnp.linalg.cholesky(balanced)
    middle = lax.linalg.triangular_solve(factor, target, left_side=True, lower=True)
    return lax.linalg.triangular_solve(factor, middle, left_side=True, lower=True, transpose_a=True)


def split_three(value):
    high = lax.reduce_precision(value, 8, 7)
    rest = value - high
    middle = lax.reduce_precision(rest, 8, 7)
    return high, middle, rest - middle


def features(positions):
    coord = positions.astype(jnp.float32)
    x, y = coord[0], coord[1]
    high, middle, low = split_three(x * x + y * y)
    one = jnp.ones_like(x)
    zero = jnp.zeros_like(x)
    pad = [zero] * (FEATURES - 8)
    near = jnp.stack([x, y, high, middle, low, one, one, one] + pad)
    far = 16.0 * jnp.stack([-2.0 * x, -2.0 * y, one, one, one, high, middle, low] + pad)
    return near.astype(jnp.bfloat16), far.astype(jnp.bfloat16)


def kernel_of(square, floor):
    square = jnp.minimum(jnp.maximum(square, floor), 16.0)
    quad = square * lax.rsqrt(square)
    remain = 4.0 - quad
    remain = remain * remain
    return (remain * remain * (quad + 1.0)).astype(jnp.bfloat16)


def block_of(near, far, floors):
    square = jnp.dot(near, far, preferred_element_type=jnp.float32)
    rows = []
    for a in range(2):
        part = square[a * TILE : (a + 1) * TILE]
        row = [kernel_of(part[:, b * TILE : (b + 1) * TILE], floors[a][b]) for b in range(2)]
        rows.append(jnp.concatenate(row, axis=1))
    return jnp.concatenate(rows, axis=0)


def times_transposed(vectors, block):
    return lax.dot_general(
        vectors, block, (((1,), (1,)), ((), ())), preferred_element_type=jnp.float32
    )


def pair_kernel(
    cells, count, near, row_pack, col_pack, row_out, col_out, own_out, col_acc, floor
):
    row_blocks, col_blocks = row_pack.shape[0], col_pack.shape[0]
    probes = row_out.shape[1]
    row_vec, col_vec = row_pack.at[:, :probes], col_pack.at[:, :probes]
    far = col_pack.at[:, probes:]
    own_blocks = own_out.shape[0]
    stride = 2 * col_blocks
    scale = AMPLITUDE / 256.0
    live = count[0]
    unroll = math.gcd(UNROLL, col_blocks)
    col_acc[...] = jnp.zeros_like(col_acc)

    @pl.loop(0, 2 * row_blocks * stride // 16)
    def _(step):
        for k in range(16):
            floor[step * 16 + k] = 16.0

    def mark(slot):
        floor[cells[slot]] = 1e-20

    whole = live // 8

    @pl.loop(0, whole)
    def _(step):
        for k in range(8):
            mark(step * 8 + k)

    @pl.loop(whole * 8, live)
    def _(slot):
        mark(slot)

    def products(i, j):
        base = 2 * i * stride + 2 * j
        floors = [[floor[base + a * stride + b] for b in range(2)] for a in range(2)]
        block = block_of(near[i], far[j], floors)
        forward = times_transposed(col_vec[j], block)
        backward = jnp.dot(row_vec[i], block, preferred_element_type=jnp.float32)
        return forward, backward

    @pl.loop(0, row_blocks)
    def _(i):
        def several(step, total):
            results = [products(i, step * unroll + k) for k in range(unroll)]
            for k, (forward, backward) in enumerate(results):
                total = total + forward
                col_acc[step * unroll + k] += backward
            return total

        start = jnp.zeros(row_out.shape[1:], jnp.float32)
        total = lax.fori_loop(0, col_blocks // unroll, several, start)
        row_out[i] = (scale * total).astype(row_out.dtype)

    row_base = lax.axis_index("col") * own_blocks
    col_base = lax.axis_index("row") * own_blocks

    @pl.loop(0, own_blocks)
    def _(t):
        block = block_of(near[row_base + t], far[col_base + t], [[1e-20, 16.0], [16.0, 1e-20]])
        own_out[t] = scale * times_transposed(col_vec[col_base + t], block)

    col_out[...] = (scale * col_acc[...]).astype(col_out.dtype)


MESH = pl.DeviceIdType.MESH


def greet(sizes):
    barrier = pltpu.get_barrier_semaphore()
    for axis, size in sizes:
        me = lax.axis_index(axis)
        for k in range(1, size):
            peer = lax.rem(me + k, size)
            pl.semaphore_signal(barrier, inc=1, device_id={axis: peer}, device_id_type=MESH)
    pl.semaphore_wait(barrier, sum(size - 1 for _, size in sizes))


class Exchange:
    def __init__(self, axis, size, source, landing, send_sem, recv_sem):
        self.axis, self.size, self.source, self.landing = axis, size, source, landing
        self.send_sem, self.recv_sem = send_sem, recv_sem
        self.me = lax.axis_index(axis)

    def copy(self, k, source, slot, peer):
        return pltpu.make_async_remote_copy(
            src_ref=source,
            dst_ref=self.landing.at[slot],
            send_sem=self.send_sem.at[k],
            recv_sem=self.recv_sem.at[k],
            device_id={self.axis: peer},
            device_id_type=MESH,
        )

    def outgoing(self, k):
        peer = lax.rem(self.me + k, self.size)
        return self.copy(k, self.source(peer), self.me, peer)

    def start(self):
        for k in range(1, self.size):
            self.outgoing(k).start()

    def wait_recv(self):
        for k in range(1, self.size):
            origin = lax.rem(self.me + self.size - k, self.size)
            self.copy(k, self.landing.at[origin], origin, origin).wait_recv()

    def wait_send(self):
        for k in range(1, self.size):
            self.outgoing(k).wait_send()


def gather_kernel(
    n_row, n_col, row_in, col_in, row_out, col_out, own_sem, row_send, row_recv, col_send, col_recv
):
    row_me, col_me = lax.axis_index("col"), lax.axis_index("row")
    own = [
        pltpu.make_async_copy(row_in, row_out.at[row_me], own_sem.at[0]),
        pltpu.make_async_copy(col_in, col_out.at[col_me], own_sem.at[1]),
    ]
    for copy in own:
        copy.start()
    greet((("row", n_row), ("col", n_col)))
    over_row = Exchange("row", n_row, lambda peer: col_in, col_out, col_send, col_recv)
    over_col = Exchange("col", n_col, lambda peer: row_in, row_out, row_send, row_recv)
    over_row.start()
    over_col.start()
    for copy in own:
        copy.wait()
    for exchange in (over_col, over_row):
        exchange.wait_recv()
        exchange.wait_send()


def image_kernel(
    n_row,
    n_col,
    row_part,
    col_part,
    own_product,
    direction,
    residual,
    applied,
    gram,
    row_land,
    col_land,
    gram_own,
    gram_half,
    gram_col,
    gram_row,
    *sems,
):
    blocks = own_product.shape[0]
    row_me, col_me = lax.axis_index("col"), lax.axis_index("row")
    greet((("row", n_row), ("col", n_col)))

    def part_of(parts):
        return lambda peer: parts.at[pl.ds(peer * blocks, blocks)]

    over_row = Exchange("row", n_row, part_of(col_part), col_land, sems[0], sems[1])
    over_col = Exchange("col", n_col, part_of(row_part), row_land, sems[2], sems[3])
    over_row.start()
    over_col.start()
    total = own_product[...]
    total += row_part[pl.ds(row_me * blocks, blocks)].astype(jnp.float32)
    total += col_part[pl.ds(col_me * blocks, blocks)].astype(jnp.float32)
    over_col.wait_recv()
    for k in range(1, n_col):
        total += row_land[lax.rem(row_me + k, n_col)].astype(jnp.float32)
    over_row.wait_recv()
    for k in range(1, n_row):
        total += col_land[lax.rem(col_me + k, n_row)].astype(jnp.float32)
    flat = jnp.concatenate([total[b] for b in range(blocks)], axis=1)
    image = NUGGET * direction[...] + flat
    applied[...] = image
    left = jnp.concatenate([image, residual[...]], axis=0)
    right = jnp.concatenate([left, direction[...]], axis=0)
    product = cross_gram_matrix(left, right)
    lanes = gram_own.shape[1] - product.shape[1]
    gram_own[...] = jnp.concatenate(
        [product, jnp.zeros((product.shape[0], lanes), jnp.float32)], axis=1
    )
    gram_over_col = Exchange("col", n_col, lambda peer: gram_own, gram_col, sems[4], sems[5])
    gram_over_col.start()
    gram_over_col.wait_recv()
    half = gram_own[...]
    for k in range(1, n_col):
        half += gram_col[lax.rem(row_me + k, n_col)]
    gram_half[...] = half
    gram_over_row = Exchange("row", n_row, lambda peer: gram_half, gram_row, sems[6], sems[7])
    gram_over_row.start()
    gram_over_row.wait_recv()
    whole = gram_half[...]
    for k in range(1, n_row):
        whole += gram_row[lax.rem(col_me + k, n_row)]
    gram[...] = whole
    for exchange in (over_row, over_col, gram_over_col, gram_over_row):
        exchange.wait_send()


def block_major(array):
    rows, points = array.shape
    return array.reshape(rows, points // BLOCK, BLOCK).transpose(1, 0, 2)


def on_device(solution_field, residual, direction, positions, tile_pairs, pair_count):
    probes, own_points = direction.shape
    own_blocks = own_points // BLOCK
    own_vec = block_major(direction.astype(jnp.bfloat16))
    near, far = features(positions)
    n_row, n_col = lax.axis_size("row"), lax.axis_size("col")
    vmem = pl.BlockSpec(memory_space=pltpu.VMEM)
    smem = pl.BlockSpec(memory_space=pltpu.SMEM)
    hbm = pl.BlockSpec(memory_space=pl.ANY)
    row_sem, col_sem = pltpu.SemaphoreType.DMA((n_col,)), pltpu.SemaphoreType.DMA((n_row,))
    row_in = jnp.concatenate([own_vec, block_major(near)], axis=1)
    col_in = jnp.concatenate([own_vec, block_major(far)], axis=1)
    row_pack, col_pack = pl.pallas_call(
        functools.partial(gather_kernel, n_row, n_col),
        out_shape=(
            jax.ShapeDtypeStruct((n_col, *row_in.shape), jnp.bfloat16),
            jax.ShapeDtypeStruct((n_row, *col_in.shape), jnp.bfloat16),
        ),
        in_specs=[vmem, vmem],
        out_specs=(hbm, hbm),
        scratch_shapes=[pltpu.SemaphoreType.DMA((2,)), row_sem, row_sem, col_sem, col_sem],
        compiler_params=pltpu.CompilerParams(collective_id=0, has_side_effects=True),
        name="gather",
    )(row_in, col_in)
    row_pack = row_pack.reshape(-1, *row_in.shape[1:])
    col_pack = col_pack.reshape(-1, *col_in.shape[1:])
    near = row_pack[:, probes:].transpose(0, 2, 1)
    row_blocks, col_blocks = row_pack.shape[0], col_pack.shape[0]
    cells = tile_pairs[0] * (2 * col_blocks) + tile_pairs[1]
    row_part, col_part, own_product = pl.pallas_call(
        pair_kernel,
        out_shape=(
            jax.ShapeDtypeStruct((row_blocks, probes, BLOCK), jnp.bfloat16),
            jax.ShapeDtypeStruct((col_blocks, probes, BLOCK), jnp.bfloat16),
            jax.ShapeDtypeStruct((own_blocks, probes, BLOCK), jnp.float32),
        ),
        in_specs=[smem, smem, vmem, vmem, vmem],
        out_specs=(vmem, vmem, vmem),
        scratch_shapes=[
            pltpu.VMEM((col_blocks, probes, BLOCK), jnp.float32),
            pltpu.SMEM((4 * row_blocks * col_blocks,), jnp.float32),
        ],
        name="pairs",
    )(cells, pair_count, near, row_pack, col_pack)
    applied, gram = pl.pallas_call(
        functools.partial(image_kernel, n_row, n_col),
        out_shape=(
            jax.ShapeDtypeStruct((probes, own_points), jnp.float32),
            jax.ShapeDtypeStruct((2 * probes, TILE), jnp.float32),
        ),
        in_specs=[vmem] * 5,
        out_specs=(vmem, vmem),
        scratch_shapes=[
            pltpu.VMEM((n_col, *own_product.shape), jnp.bfloat16),
            pltpu.VMEM((n_row, *own_product.shape), jnp.bfloat16),
            pltpu.VMEM((2 * probes, TILE), jnp.float32),
            pltpu.VMEM((2 * probes, TILE), jnp.float32),
            pltpu.VMEM((n_col, 2 * probes, TILE), jnp.float32),
            pltpu.VMEM((n_row, 2 * probes, TILE), jnp.float32),
            col_sem,
            col_sem,
            row_sem,
            row_sem,
            row_sem,
            row_sem,
            col_sem,
            col_sem,
        ],
        compiler_params=pltpu.CompilerParams(collective_id=1, has_side_effects=True),
        name="image",
    )(row_part, col_part, own_product, direction, residual)
    square, image_resid = gram[:probes, :probes], gram[:probes, probes : 2 * probes]
    norm_old = gram[probes:, probes : 2 * probes]
    curvature = gram[:probes, 2 * probes : 3 * probes].T
    crossing = gram[probes:, 2 * probes : 3 * probes].T
    step_size = symmetric_solve(curvature, crossing)
    residual_next = residual - apply_left(step_size, applied)
    shifted = jnp.dot(step_size.T, image_resid, precision=HIGHEST)
    quadratic = jnp.dot(
        step_size.T, jnp.dot(square, step_size, precision=HIGHEST), precision=HIGHEST
    )
    norm_new = norm_old - shifted - shifted.T + quadratic
    solution_next = solution_field + apply_left(step_size, direction)
    mix_weight = symmetric_solve(norm_old, norm_new)
    direction_next = residual_next + apply_left(mix_weight, direction)
    return (solution_next, residual_next, direction_next)


def solution(mesh):
    whole = P(None, ("row", "col"))
    return jax.shard_map(
        on_device,
        mesh=mesh,
        in_specs=(whole, whole, whole, whole, whole, P(("row", "col"))),
        out_specs=(whole, whole, whole),
        check_vma=False,
    )
```
